32 devices in a mesh: seq: 8 (over z, x), head: 4 (over y, core).
Axes of the slice: x: 2, y: 2, z: 4, core: 2. Of those that a mesh axis runs over, the one named last changes fastest.
Arguments:
- queries: bfloat16 [2048, 2048], P('seq', 'head'), may hold values from -1.75 to 1.75
- keys: bfloat16 [2048, 2048], P('seq', 'head'), may hold values from -1.75 to 1.75
- values: bfloat16 [2048, 2048], P('seq', 'head'), may hold values from -6 to 6
- level_table: float32 [16, 16], P(None, 'head'), may hold values from 0.05 to 1
- level_code: int32 [2048, 6], P('seq'), may hold values from 0 to 15
- out_weight: bfloat16 [2048, 2048], P('head'), may hold values from -0.125 to 0.125
- cotangent: bfloat16 [2048, 2048], P('seq', 'head'), may hold values from -8 to 8
Outputs:
- mixed: bfloat16 [2048, 2048], P('seq', 'head')
- out_weight_grad: float32 [2048, 2048], P('seq', 'head')
- query_grad: bfloat16 [2048, 2048], P('seq', 'head')
- key_grad: bfloat16 [2048, 2048], P('seq', 'head')
- value_grad: bfloat16 [2048, 2048], P('seq', 'head')
- table_grad: float32 [16, 16], P(None, 'head')
The draws below stay inside these ranges and needn't reach their ends.
All inputs are finite; a program needn't handle non-finite values.
Results may differ from the reference program's by a relative error of at most 0.015.
Values may be sent and summed in bfloat16 or wider, within the bound.
No kernel may reach another device: no remote copies, remote signals or barrier semaphores. Data moves between devices by JAX's collectives and lax.ppermute only.
A program may use at most 128 MiB of HBM per device.

```python
import math
import jax
import jax.numpy as jnp
from jax import lax

WIDTH = 2048
HEADS = 16
HEAD_DIM = 128
SPAN = 64
CODES = 16
LEVELS = 6
TOKENS = 2048
N_HEAD = 4


def plant(drawn, stream_key, low, high):
    shape = drawn.shape
    place = [jax.random.randint(jax.random.fold_in(stream_key, axis), (), 0, shape[axis]) for axis in range(len(shape))]
    drawn = drawn.at[tuple(place)].set(low)
    longest = shape.index(max(shape))
    place[longest] = (place[longest] + 1) % shape[longest]
    return drawn.at[tuple(place)].set(high)


def raised(entries, own_key, source, target, blocks, factor):
    def block_of(position):
        return (jnp.arange(entries.shape[position]) // (entries.shape[position] // blocks)).reshape((-1,) + (1,) * (entries.ndim - 1 - position))

    one_side = jax.random.permutation(own_key, blocks)[block_of(target)]
    second = (block_of(target) + blocks // 2) % blocks
    return jnp.where((block_of(source) == one_side) | (block_of(source) == second), factor * entries, entries)


def block_levels(stream_key, extent, split, smallest, high):
    level, own = 1.0, jax.random.fold_in(stream_key, 6)
    for dim, parts in split:
        draws = jnp.exp(jax.random.uniform(jax.random.fold_in(own, dim), (parts,), jnp.float32, smallest / len(split), high / len(split)))
        level = level * jnp.repeat(draws, extent[dim] // parts).reshape([-1 if axis == dim else 1 for axis in range(len(extent))])
    return level


def centred(key, shape, width, limit, shards=(), held_as=jnp.bfloat16):
    drawn = jax.random.normal(key, shape, jnp.float32) * width
    if len(shards) > 0:
        drawn = block_levels(key, shape, shards, -0.22, 0.18) * drawn
    return jnp.clip(drawn, min=-limit, max=limit).astype(held_as)


def noise_with(key, dims, spread, limit, shards, heavy, held_as=jnp.bfloat16):
    values = spread * jax.random.normal(key, dims, jnp.float32)
    if shards:
        values = values * block_levels(key, dims, shards, -0.22, 0.18)
    return jnp.clip(raised(values, jax.random.fold_in(key, 3), *heavy), -limit, limit).astype(held_as)


def setup_inputs(seed: int = 0) -> dict:
    streams_of = jax.random.split(jax.random.key(seed), 8)
    return {
        "queries": centred(streams_of[0], (TOKENS, HEADS * HEAD_DIM), 0.3, 1.75, ((0, 8), (1, 4))),
        "keys": centred(streams_of[1], (TOKENS, HEADS * HEAD_DIM), 0.3, 1.75, ((0, 8), (1, 4))),
        "values": centred(streams_of[2], (TOKENS, HEADS * HEAD_DIM), 1.0, 6.0, ((0, 8), (1, 4))),
        "level_table": jnp.clip(jnp.exp(math.log(1.0) - 2.9957323 * jax.random.uniform(streams_of[3], (CODES, HEADS), jnp.float32) ** block_levels(streams_of[3], (CODES, HEADS), ((1, 4),), -0.2, 0.2)), 0.05, 1.0),
        "level_code": plant(jax.random.randint(streams_of[4], (TOKENS, LEVELS), 0, CODES), jax.random.fold_in(streams_of[4], 1), 0, CODES - 1).astype(jnp.int32),
        "out_weight": centred(streams_of[5], (HEADS * HEAD_DIM, WIDTH), (HEADS * HEAD_DIM) ** -0.5, 0.125, ((0, 4),)),
        "cotangent": noise_with(streams_of[6], (TOKENS, WIDTH), 1.0, 8.0, ((0, 8), (1, 4)), (0, 1, 8, 2.0)),
    }


HIGHEST_PRECISION = lax.Precision.HIGHEST

def level_attention(q_head, k_head, v_head, lam_head):
    span_total = q_head.shape[0] // SPAN
    q_four = q_head.reshape(span_total, SPAN, HEAD_DIM)
    k_four = k_head.reshape(span_total, SPAN, HEAD_DIM)
    v_four = v_head.reshape(span_total, SPAN, HEAD_DIM)
    causal = (jnp.arange(SPAN)[:, None] >= jnp.arange(SPAN)[None, :]).astype(q_head.dtype)
    scores = jnp.einsum('ncd,nsd->ncs', q_four, k_four, precision=HIGHEST_PRECISION) * causal
    within = jnp.einsum('ncs,nse->nce', scores, v_four, precision=HIGHEST_PRECISION).reshape(q_head.shape)
    result = within * (lam_head[:, 0:1] / math.sqrt(SPAN))
    states = jnp.einsum('ncd,nce->nde', k_four, v_four, precision=HIGHEST_PRECISION)
    for bit_index in range(LEVELS - 1):
        group_size = 2 ** (bit_index + 1)
        half_size = group_size // 2
        group_count = span_total // group_size
        lower_state = lax.optimization_barrier(jnp.sum(states.reshape(group_count, group_size, HEAD_DIM, HEAD_DIM)[:, :half_size], axis=1))
        upper_queries = q_four.reshape(group_count, group_size, SPAN, HEAD_DIM)[:, half_size:]
        level_reads = jnp.einsum('gjcd,gde->gjce', upper_queries, lower_state, precision=HIGHEST_PRECISION)
        placed = jnp.concatenate([jnp.zeros_like(level_reads), level_reads], axis=1).reshape(q_head.shape)
        result = result + placed * (lam_head[:, bit_index + 1:bit_index + 2] / math.sqrt(SPAN * 2 ** bit_index))
    return result

def head_major(array):
    return array.reshape(TOKENS, HEADS, HEAD_DIM).transpose(1, 0, 2)

def reference(queries, keys, values, level_table, level_code, out_weight, cotangent):
    lam = jnp.take(level_table, level_code, axis=0)
    lam_heads = jnp.transpose(lam, (2, 0, 1))
    stacked = (head_major(queries), head_major(keys), head_major(values), lam_heads)

    def forward_head(head_items):
        q_head, k_head, v_head, lam_head = head_items
        return level_attention(q_head.astype(jnp.float32), k_head.astype(jnp.float32), v_head.astype(jnp.float32), lam_head)
    attention = lax.map(forward_head, stacked)
    attn_rows = attention.transpose(1, 0, 2).reshape(TOKENS, HEADS * HEAD_DIM).astype(jnp.bfloat16)
    group_cols = HEADS * HEAD_DIM // N_HEAD
    head_total = jnp.zeros((TOKENS, WIDTH), jnp.float32)
    for group_index in range(N_HEAD):
        partial_value = jnp.dot(attn_rows[:, group_index * group_cols:(group_index + 1) * group_cols], out_weight[group_index * group_cols:(group_index + 1) * group_cols], preferred_element_type=jnp.float32)
        head_total = head_total + partial_value.astype(jnp.bfloat16).astype(jnp.float32)
    mixed = head_total.astype(jnp.bfloat16)
    grad_attn = jnp.dot(cotangent, out_weight.T, preferred_element_type=jnp.float32).astype(jnp.bfloat16)
    out_weight_grad = jnp.dot(cotangent.T, attn_rows, preferred_element_type=jnp.float32) / math.sqrt(TOKENS)

    def backward_head(head_items):
        q_head, k_head, v_head, lam_head, grad_head = head_items
        unused, pullback = jax.vjp(level_attention, q_head.astype(jnp.float32), k_head.astype(jnp.float32), v_head.astype(jnp.float32), lam_head)
        return pullback(grad_head.astype(jnp.float32))
    q_grads, k_grads, v_grads, lam_grads = lax.map(backward_head, stacked + (head_major(grad_attn),))

    def rows_back(array):
        return array.transpose(1, 0, 2).reshape(TOKENS, HEADS * HEAD_DIM).astype(jnp.bfloat16)
    one_hot = (level_code[:, :, None] == jnp.arange(CODES, dtype=jnp.int32)[None, None, :]).astype(jnp.float32)
    table_grad = jnp.einsum('htl,tlc->ch', lam_grads, one_hot, precision=HIGHEST_PRECISION) / math.sqrt(TOKENS * LEVELS)
    return (mixed, out_weight_grad, rows_back(q_grads), rows_back(k_grads), rows_back(v_grads), table_grad)
```

```python
import functools
import math

import jax
import jax.numpy as jnp
from jax import lax
from jax.experimental import pallas as pl
from jax.experimental.pallas import tpu as pltpu
from jax.sharding import PartitionSpec as P

SPAN = 64
F32 = jnp.float32
BF16 = jnp.bfloat16
VMEM_LIMIT = 24 * 1024 * 1024

VMEM_SPEC = pl.BlockSpec(memory_space=pltpu.VMEM)
SMEM_SPEC = pl.BlockSpec(memory_space=pltpu.SMEM)


def nn(left, right):
    return lax.dot_general(left, right, (((1,), (0,)), ((), ())), preferred_element_type=F32)


def nt(left, right):
    return lax.dot_general(left, right, (((1,), (1,)), ((), ())), preferred_element_type=F32)


def tn(left, right):
    return lax.dot_general(left, right, (((0,), (0,)), ((), ())), preferred_element_type=F32)


def local_call(body, outs, ins, scalars=0, flops=0, scratch=(), name=None):
    moved = sum(math.prod(o.shape) * o.dtype.itemsize for o in outs)
    moved += sum(math.prod(a.shape) * a.dtype.itemsize for a in ins)
    return pl.pallas_call(
        body,
        out_shape=tuple(outs),
        in_specs=[SMEM_SPEC] * scalars + [VMEM_SPEC] * (len(ins) - scalars),
        out_specs=tuple(VMEM_SPEC for _ in outs),
        scratch_shapes=scratch,
        compiler_params=pltpu.CompilerParams(vmem_limit_bytes=VMEM_LIMIT),
        cost_estimate=pl.CostEstimate(flops=flops, bytes_accessed=moved, transcendentals=0),
        name=name,
    )(*ins)


def shaped(shape, dtype):
    return jax.ShapeDtypeStruct(shape, dtype)


def state_body(heads, k_ref, v_ref, d_ref):
    size = k_ref.shape[1] // heads
    for h in range(heads):
        cols = slice(h * size, (h + 1) * size)
        d_ref[h * size : (h + 1) * size, :] = tn(k_ref[:, cols], v_ref[:, cols]).astype(BF16)


def coef_body(levels, scales, code_ref, table_ref, coef_ref, hot_ref):
    heads, codes = table_ref.shape
    table = table_ref[...]
    high = table.astype(BF16)
    low = (table - high.astype(F32)).astype(BF16)
    tokens = code_ref.shape[1]
    row = lax.broadcasted_iota(jnp.int32, (codes, tokens), 0)
    for l in range(levels):
        hot = jnp.where(row == code_ref[l : l + 1, :], 1.0, 0.0).astype(BF16)
        hot_ref[l * codes : (l + 1) * codes, :] = hot
        lam = lax.dot_general(hot, high, (((0,), (1,)), ((), ())), preferred_element_type=F32)
        lam = lam + lax.dot_general(hot, low, (((0,), (1,)), ((), ())), preferred_element_type=F32)
        coef_ref[:, l * heads : (l + 1) * heads] = lam * scales[l]


def grad_body(heads, local_levels, levels, count, *refs):
    head_ref = refs[0]
    blocks = refs[1 : 1 + count]
    w_ref, q_ref, coef_ref, g_ref, full_ref, t_ref = refs[1 + count :]
    me = head_ref[0]
    width = blocks[0].shape[1]
    size = q_ref.shape[1] // heads
    total = None
    for m in range(count):
        start = pl.multiple_of((me ^ m) * width, width)
        block = blocks[m][...]
        full_ref[:, pl.ds(start, width)] = block
        part = nt(block, w_ref[:, pl.ds(start, width)])
        total = part if total is None else total + part
    g = total.astype(BF16)
    g_ref[...] = g
    for l in range(local_levels, levels):
        for h in range(heads):
            cols = slice(h * size, (h + 1) * size)
            scaled = (g[:, cols].astype(F32) * coef_ref[:, l * heads + h : l * heads + h + 1]).astype(BF16)
            t_ref[l - local_levels, h * size : (h + 1) * size, :] = tn(q_ref[:, cols], scaled).astype(BF16)


def level_masks(tokens, local_levels):
    row = lax.broadcasted_iota(jnp.int32, (tokens, tokens), 0)
    col = lax.broadcasted_iota(jnp.int32, (tokens, tokens), 1)
    apart = (row // SPAN) ^ (col // SPAN)
    causal = col <= row
    masks = [causal & (apart == 0)]
    for l in range(1, local_levels):
        masks.append(causal & ((apart >> (l - 1)) == 1))
    return masks


def inner_body(heads, local_levels, scales, q_ref, k_ref, v_ref, g_ref, coef_ref,
               attn_ref, dq_ref, dk_ref, dv_ref, lev_ref):
    tokens = q_ref.shape[0]
    size = q_ref.shape[1] // heads
    masks = level_masks(tokens, local_levels)
    lane = lax.broadcasted_iota(jnp.int32, lev_ref.shape, 1)
    lev = jnp.zeros(lev_ref.shape, F32)
    for h in range(heads):
        cols = slice(h * size, (h + 1) * size)
        q, k, v, g = q_ref[:, cols], k_ref[:, cols], v_ref[:, cols], g_ref[:, cols]
        weight = jnp.zeros((tokens, tokens), F32)
        for l in range(local_levels):
            weight = jnp.where(masks[l], coef_ref[:, l * heads + h : l * heads + h + 1], weight)
        scores = nt(q, k)
        grads = nt(g, v)
        both = scores * grads
        for l in range(local_levels):
            part = jnp.sum(jnp.where(masks[l], both, 0.0), axis=1, keepdims=True) * scales[l]
            lev = jnp.where(lane == l * heads + h, part, lev)
        scores = (scores * weight).astype(BF16)
        grads = (grads * weight).astype(BF16)
        attn_ref[:, cols] = nn(scores, v)
        dq_ref[:, cols] = nn(grads, k)
        dk_ref[:, cols] = tn(grads, q)
        dv_ref[:, cols] = tn(scores, g)
    lev_ref[...] = lev


def outer_body(heads, local_levels, levels, scales, norm, seq_ref, q_ref, g_ref, coef_ref, hot_ref,
               attn_in, dq_in, lev_ref, *rest):
    states = rest[: levels - local_levels]
    attn_ref, dq_ref, table_ref = rest[levels - local_levels :]
    me = seq_ref[0]
    size = q_ref.shape[1] // heads
    codes = table_ref.shape[0]
    lane = lax.broadcasted_iota(jnp.int32, lev_ref.shape, 1)
    lev = lev_ref[...]
    for h in range(heads):
        cols = slice(h * size, (h + 1) * size)
        q, g = q_ref[:, cols], g_ref[:, cols]
        qf = q.astype(F32)
        attn = attn_in[:, cols]
        dq = dq_in[:, cols]
        for l in range(local_levels, levels):
            b = l - local_levels
            owned = ((me >> b) & 1).astype(F32)
            state = states[b][h * size : (h + 1) * size, :]
            coef = coef_ref[:, l * heads + h : l * heads + h + 1] * owned
            attn = attn + coef * nn(q, state)
            back = nt(g, state)
            dq = dq + coef * back
            part = jnp.sum(qf * back, axis=1, keepdims=True) * (owned * scales[l])
            lev = jnp.where(lane == l * heads + h, part, lev)
        attn_ref[:, cols] = attn.astype(BF16)
        dq_ref[:, cols] = dq.astype(BF16)
    high = lev.astype(BF16)
    low = (lev - high.astype(F32)).astype(BF16)
    total = jnp.zeros((codes, heads), F32)
    for l in range(levels):
        hot = hot_ref[l * codes : (l + 1) * codes, :]
        pick = slice(l * heads, (l + 1) * heads)
        total = total + nn(hot, high[:, pick]) + nn(hot, low[:, pick])
    table_ref[...] = total * norm


def weight_body(masks_a, masks_b, scale, seq_ref, full_ref, attn_ref, a_ref, b_ref, *scratch):
    me = seq_ref[0]
    rows, half = a_ref.shape[1:]
    for masks, out_ref, cols in ((masks_a, a_ref, slice(0, half)), (masks_b, b_ref, slice(half, 2 * half))):
        if scratch:
            scratch[0][...] = tn(full_ref[...], attn_ref[:, cols]) * scale
        for n, m in enumerate(masks):
            start = pl.multiple_of((me ^ m) * rows, rows)
            if scratch:
                out_ref[n] = scratch[0][pl.ds(start, rows), :].astype(out_ref.dtype)
            else:
                part = tn(full_ref[:, pl.ds(start, rows)], attn_ref[:, cols])
                out_ref[n] = (part * scale).astype(out_ref.dtype)


def mixed_body(masks, head_ref, attn_ref, w_ref, o_ref):
    me = head_ref[0]
    width = o_ref.shape[2]
    for n, m in enumerate(masks):
        start = pl.multiple_of((me ^ m) * width, width)
        o_ref[n] = nn(attn_ref[...], w_ref[:, pl.ds(start, width)]).astype(BF16)


def final_body(heads, k_ref, v_ref, u_ref, dk_in, dv_in, dk_ref, dv_ref):
    size = k_ref.shape[1] // heads
    for h in range(heads):
        cols = slice(h * size, (h + 1) * size)
        u = u_ref[h * size : (h + 1) * size, :]
        dk_ref[:, cols] = (dk_in[:, cols] + nt(v_ref[:, cols], u)).astype(BF16)
        dv_ref[:, cols] = (dv_in[:, cols] + nn(k_ref[:, cols], u)).astype(BF16)


def swap(value, axis, bit):
    pairs = [(i, i ^ (1 << bit)) for i in range(lax.axis_size(axis))]
    return lax.ppermute(value, axis, pairs)


def one_way(value, axis, bit, up):
    n = lax.axis_size(axis)
    pairs = [(i, i ^ (1 << bit)) for i in range(n) if ((i >> bit) & 1) == (0 if up else 1)]
    return lax.ppermute(value, axis, pairs)


def bit_order(bits, order):
    masks = [0]
    for bit in order:
        masks = [m for m in masks] + [m | (1 << bit) for m in masks]
    return masks


def reduce_blocks(order, send, keep):
    for n, bit in enumerate(order):
        got = swap(send, "seq", bit).astype(F32)
        total = keep.astype(F32) + got
        if n + 1 == len(order):
            return total[0]
        half = total.shape[0] // 2
        keep = total[:half]
        send = total[half:].astype(BF16)


def per_device(queries, keys, values, level_table, level_code, out_weight, cotangent):
    tokens, cols = queries.shape
    heads = level_table.shape[1]
    codes = level_table.shape[0]
    size = cols // heads
    width = out_weight.shape[1]
    spans = tokens // SPAN
    local_bits = spans.bit_length() - 1
    seq_count = lax.axis_size("seq")
    seq_bits = seq_count.bit_length() - 1
    head_count = lax.axis_size("head")
    head_bits = head_count.bit_length() - 1
    local_levels = 1 + local_bits
    levels = local_levels + seq_bits
    scales = [1.0 / math.sqrt(SPAN * 2 ** max(l - 1, 0)) for l in range(levels)]
    seq_me = lax.axis_index("seq").astype(jnp.int32)
    head_me = lax.axis_index("head").astype(jnp.int32)
    seq_one = seq_me.reshape(1)
    head_one = head_me.reshape(1)

    blocks = {0: cotangent}
    for bit in reversed(range(head_bits)):
        for m in list(blocks):
            blocks[m | (1 << bit)] = swap(blocks[m], "head", bit)

    (state,) = local_call(
        functools.partial(state_body, heads),
        [shaped((cols, size), BF16)],
        [keys, values],
        flops=2 * tokens * cols * size,
        name="state",
    )
    coef, hot = local_call(
        functools.partial(coef_body, levels, scales),
        [shaped((tokens, levels * heads), F32), shaped((levels * codes, tokens), BF16)],
        [level_code.T, level_table.T],
        flops=4 * tokens * levels * codes * heads,
        name="coef",
    )
    found = []
    block_state = state
    for bit in range(seq_bits):
        if bit == seq_bits - 1:
            found.append(one_way(block_state, "seq", bit, True))
        else:
            got = swap(block_state, "seq", bit)
            found.append(got)
            block_state = (block_state.astype(F32) + got.astype(F32)).astype(BF16)

    g, full, terms = local_call(
        functools.partial(grad_body, heads, local_levels, levels, head_count),
        [
            shaped((tokens, cols), BF16),
            shaped((tokens, width), BF16),
            shaped((seq_bits, cols, size), BF16),
        ],
        [head_one] + [blocks[m] for m in range(head_count)] + [out_weight, queries, coef],
        scalars=1,
        flops=2 * tokens * cols * width,
        name="grad",
    )
    gathered = None
    for bit in range(seq_bits):
        if bit == seq_bits - 1:
            got = one_way(terms, "seq", bit, False)
            first = got[0].astype(F32)
        else:
            got = swap(terms, "seq", bit)
            first = got[0].astype(F32) * (1 - ((seq_me >> bit) & 1)).astype(F32)
            terms = (terms[1:].astype(F32) + got[1:].astype(F32)).astype(BF16)
        gathered = first if gathered is None else gathered + first
    gathered = gathered.astype(BF16)

    attn_in, dq_in, dk_in, dv_in, lev = local_call(
        functools.partial(inner_body, heads, local_levels, scales),
        [shaped((tokens, cols), F32)] * 4 + [shaped((tokens, 128 * pl.cdiv(levels * heads, 128)), F32)],
        [queries, keys, values, g, coef],
        flops=12 * tokens * tokens * cols,
        name="inner",
    )
    table_norm = 1.0 / math.sqrt(tokens * seq_count * levels)
    attn, query_grad, table_part = local_call(
        functools.partial(outer_body, heads, local_levels, levels, scales, table_norm),
        [shaped((tokens, cols), BF16), shaped((tokens, cols), BF16), shaped((codes, heads), F32)],
        [seq_one, queries, g, coef, hot, attn_in, dq_in, lev] + found,
        scalars=1,
        flops=4 * tokens * cols * size * seq_bits,
        name="outer",
    )

    weight_norm = 1.0 / math.sqrt(tokens * seq_count)
    order_a = list(range(seq_bits))
    order_b = order_a[1:] + order_a[:1]
    masks_a = bit_order(seq_bits, reversed(order_a))
    masks_b = bit_order(seq_bits, reversed(order_b))
    half = seq_count // 2
    rows = width // seq_count

    def weight_part(low, high, dtype, name):
        return local_call(
            functools.partial(weight_body, masks_a[low:high], masks_b[low:high], weight_norm),
            [shaped((high - low, rows, cols // 2), dtype)] * 2,
            [seq_one, full, attn],
            scalars=1,
            flops=tokens * cols * width,
            scratch=[pltpu.VMEM((width, cols // 2), F32)] if rows % 128 else [],
            name=name,
        )

    a_send, b_send = weight_part(half, seq_count, BF16, "weight_send")
    a_keep, b_keep = weight_part(0, half, BF16, "weight_keep")
    weight_a = reduce_blocks(order_a, a_send, a_keep)
    weight_b = reduce_blocks(order_b, b_send, b_keep)
    out_weight_grad = jnp.concatenate([weight_a, weight_b], axis=1)

    masks_m = bit_order(head_bits, reversed(range(head_bits)))
    (partial_value,) = local_call(
        functools.partial(mixed_body, masks_m),
        [shaped((head_count, tokens, width // head_count), BF16)],
        [head_one, attn, out_weight],
        scalars=1,
        flops=2 * tokens * cols * width,
        name="mixed",
    )
    keep, send = partial_value[: head_count // 2], partial_value[head_count // 2 :]
    for bit in range(head_bits):
        total = keep.astype(F32) + swap(send, "head", bit).astype(F32)
        if bit + 1 < head_bits:
            part = total.shape[0] // 2
            keep, send = total[:part], total[part:].astype(BF16)
    mixed = total[0].astype(BF16)

    table_grad = table_part
    for bit in range(seq_bits):
        table_grad = table_grad + swap(table_grad, "seq", bit)

    key_grad, value_grad = local_call(
        functools.partial(final_body, heads),
        [shaped((tokens, cols), BF16)] * 2,
        [keys, values, gathered, dk_in, dv_in],
        flops=4 * tokens * cols * size,
        name="final",
    )
    return mixed, out_weight_grad, query_grad, key_grad, value_grad, table_grad


def solution(mesh):
    placed = (
        P("seq", "head"),
        P("seq", "head"),
        P("seq", "head"),
        P(None, "head"),
        P("seq", None),
        P("head", None),
        P("seq", "head"),
    )
    return jax.shard_map(
        per_device,
        mesh=mesh,
        in_specs=placed,
        out_specs=(
            P("seq", "head"),
            P("seq", "head"),
            P("seq", "head"),
            P("seq", "head"),
            P("seq", "head"),
            P(None, "head"),
        ),
        check_vma=False,
    )
```

```python
import functools
import math

import jax
import jax.numpy as jnp
from jax import lax
from jax.experimental import pallas as pl
from jax.experimental.pallas import tpu as pltpu
from jax.sharding import PartitionSpec as P

SPAN = 64
F32 = jnp.float32
BF16 = jnp.bfloat16
VMEM_LIMIT = None

VMEM_SPEC = pl.BlockSpec(memory_space=pltpu.VMEM)
SMEM_SPEC = pl.BlockSpec(memory_space=pltpu.SMEM)


def nn(left, right):
    return lax.dot_general(left, right, (((1,), (0,)), ((), ())), preferred_element_type=F32)


def nt(left, right):
    return lax.dot_general(left, right, (((1,), (1,)), ((), ())), preferred_element_type=F32)


def tn(left, right):
    return lax.dot_general(left, right, (((0,), (0,)), ((), ())), preferred_element_type=F32)


def local_call(body, outs, ins, scalars=0, flops=0, scratch=(), name=None):
    moved = sum(math.prod(o.shape) * o.dtype.itemsize for o in outs)
    moved += sum(math.prod(a.shape) * a.dtype.itemsize for a in ins)
    return pl.pallas_call(
        body,
        out_shape=tuple(outs),
        in_specs=[SMEM_SPEC] * scalars + [VMEM_SPEC] * (len(ins) - scalars),
        out_specs=tuple(VMEM_SPEC for _ in outs),
        scratch_shapes=scratch,
        compiler_params=pltpu.CompilerParams(vmem_limit_bytes=VMEM_LIMIT),
        cost_estimate=pl.CostEstimate(flops=flops, bytes_accessed=moved, transcendentals=0),
        name=name,
    )(*ins)


def shaped(shape, dtype):
    return jax.ShapeDtypeStruct(shape, dtype)


def state_body(heads, k_ref, v_ref, d_ref):
    size = k_ref.shape[1] // heads
    for h in range(heads):
        cols = slice(h * size, (h + 1) * size)
        d_ref[h * size : (h + 1) * size, :] = tn(k_ref[:, cols], v_ref[:, cols]).astype(BF16)


def coef_body(levels, scales, code_ref, table_ref, coef_ref, hot_ref):
    heads, codes = table_ref.shape
    table = table_ref[...]
    high = table.astype(BF16)
    low = (table - high.astype(F32)).astype(BF16)
    tokens = code_ref.shape[1]
    row = lax.broadcasted_iota(jnp.int32, (codes, tokens), 0)
    for l in range(levels):
        hot = jnp.where(row == code_ref[l : l + 1, :], 1.0, 0.0).astype(BF16)
        hot_ref[l * codes : (l + 1) * codes, :] = hot
        lam = lax.dot_general(hot, high, (((0,), (1,)), ((), ())), preferred_element_type=F32)
        lam = lam + lax.dot_general(hot, low, (((0,), (1,)), ((), ())), preferred_element_type=F32)
        coef_ref[:, l * heads : (l + 1) * heads] = lam * scales[l]


def grad_body(heads, local_levels, levels, count, group, rows, *refs):
    head_ref, seq_ref = refs[:2]
    blocks = refs[2 : 2 + count]
    w_ref, q_ref, coef_ref, g_ref, t_ref = refs[2 + count : 7 + count]
    picked = refs[7 + count : -1]
    full_ref = refs[-1]
    me = head_ref[0]
    width = blocks[0].shape[1]
    size = q_ref.shape[1] // heads
    total = None
    for m in range(count):
        start = pl.multiple_of((me ^ m) * width, width)
        block = blocks[m][...]
        full_ref[:, pl.ds(start, width)] = block
        part = nt(block, w_ref[:, pl.ds(start, width)])
        total = part if total is None else total + part
    g = total.astype(BF16)
    g_ref[...] = g
    for l in range(local_levels, levels):
        for h in range(heads):
            cols = slice(h * size, (h + 1) * size)
            scaled = (g[:, cols].astype(F32) * coef_ref[:, l * heads + h : l * heads + h + 1]).astype(BF16)
            t_ref[l - local_levels, h * size : (h + 1) * size, :] = tn(q_ref[:, cols], scaled).astype(BF16)
    if len(picked) == 1:
        picked[0][...] = full_ref[...]
        return
    low = seq_ref[0] & (group - 1)
    for m in range(group):
        for n in range(picked[m].shape[1] // rows):
            start = pl.multiple_of((n * group + (low ^ m)) * rows, rows)
            picked[m][:, n * rows : (n + 1) * rows] = full_ref[:, pl.ds(start, rows)]


def level_masks(tokens, local_levels):
    row = lax.broadcasted_iota(jnp.int32, (tokens, tokens), 0)
    col = lax.broadcasted_iota(jnp.int32, (tokens, tokens), 1)
    apart = (row // SPAN) ^ (col // SPAN)
    causal = col <= row
    masks = [causal & (apart == 0)]
    for l in range(1, local_levels):
        masks.append(causal & ((apart >> (l - 1)) == 1))
    return masks


def inner_body(heads, local_levels, scales, q_ref, k_ref, v_ref, g_ref, coef_ref,
               attn_ref, dq_ref, dk_ref, dv_ref, lev_ref):
    tokens = q_ref.shape[0]
    size = q_ref.shape[1] // heads
    masks = level_masks(tokens, local_levels)
    lane = lax.broadcasted_iota(jnp.int32, lev_ref.shape, 1)
    lev = jnp.zeros(lev_ref.shape, F32)
    for h in range(heads):
        cols = slice(h * size, (h + 1) * size)
        q, k, v, g = q_ref[:, cols], k_ref[:, cols], v_ref[:, cols], g_ref[:, cols]
        weight = jnp.zeros((tokens, tokens), F32)
        for l in range(local_levels):
            weight = jnp.where(masks[l], coef_ref[:, l * heads + h : l * heads + h + 1], weight)
        scores = nt(q, k)
        grads = nt(g, v)
        both = scores * grads
        for l in range(local_levels):
            part = jnp.sum(jnp.where(masks[l], both, 0.0), axis=1, keepdims=True) * scales[l]
            lev = jnp.where(lane == l * heads + h, part, lev)
        scores = (scores * weight).astype(BF16)
        grads = (grads * weight).astype(BF16)
        attn_ref[:, cols] = nn(scores, v)
        dq_ref[:, cols] = nn(grads, k)
        dk_ref[:, cols] = tn(grads, q)
        dv_ref[:, cols] = tn(scores, g)
    lev_ref[...] = lev


def outer_body(heads, local_levels, which, levels, scales, norm, seq_ref, q_ref, g_ref, coef_ref,
               attn_in, dq_in, lev_in, *rest):
    states = rest[: len(which)]
    rest = rest[len(which) :]
    me = seq_ref[0]
    tokens = q_ref.shape[0]
    size = q_ref.shape[1] // heads
    last = norm is not None
    if last:
        hot_ref, attn_ref, dq_ref = rest
    else:
        attn_ref, dq_ref, lev_ref = rest
    lane = lax.broadcasted_iota(jnp.int32, lev_in.shape, 1)
    lev = lev_in[...]
    for h in range(heads):
        cols = slice(h * size, (h + 1) * size)
        q, g = q_ref[:, cols], g_ref[:, cols]
        qf = q.astype(F32)
        attn = attn_in[:, cols]
        dq = dq_in[:, cols]
        for n, l in enumerate(which):
            owned = ((me >> (l - local_levels)) & 1).astype(F32)
            state = states[n][h * size : (h + 1) * size, :]
            coef = coef_ref[:, l * heads + h : l * heads + h + 1] * owned
            attn = attn + coef * nn(q, state)
            back = nt(g, state)
            dq = dq + coef * back
            part = jnp.sum(qf * back, axis=1, keepdims=True) * (owned * scales[l])
            lev = jnp.where(lane == l * heads + h, part, lev)
        attn_ref[:tokens, cols] = attn.astype(attn_ref.dtype)
        dq_ref[:, cols] = dq.astype(dq_ref.dtype)
    if not last:
        lev_ref[...] = lev
        return
    codes = attn_ref.shape[0] - tokens
    high = lev.astype(BF16)
    low = (lev - high.astype(F32)).astype(BF16)
    total = jnp.zeros((codes, heads), F32)
    for l in range(levels):
        hot = hot_ref[l * codes : (l + 1) * codes, :]
        pick = slice(l * heads, (l + 1) * heads)
        total = total + nn(hot, high[:, pick]) + nn(hot, low[:, pick])
    total = total * norm
    high = total.astype(BF16)
    low = total - high.astype(F32)
    attn_ref[tokens:, :] = jnp.zeros((codes, attn_ref.shape[1]), BF16)
    attn_ref[tokens:, :heads] = high
    attn_ref[tokens:, heads : 2 * heads] = low.astype(BF16)


def weight_body(masks, scale, group_bits, heads, seq_ref, *refs):
    count = 1 << group_bits
    picked, attns = refs[:count], refs[count : 2 * count]
    out_ref, table_ref = refs[2 * count : 2 * count + 2]
    scratch = refs[2 * count + 2 :]
    me = seq_ref[0] >> group_bits
    rows = out_ref.shape[1]
    tokens = picked[0].shape[0]
    codes = table_ref.shape[0]

    def product(cols):
        total = None
        for m in range(count):
            part = tn(picked[m][:, cols], attns[m][:tokens, :])
            total = part if total is None else total + part
        return total * scale

    if scratch:
        scratch[0][...] = product(slice(None))
    for n, m in enumerate(masks):
        start = pl.multiple_of((me ^ m) * rows, rows)
        total = scratch[0][pl.ds(start, rows), :] if scratch else product(pl.ds(start, rows))
        out_ref[n] = total.astype(out_ref.dtype)
    table = jnp.zeros((codes, heads), F32)
    for m in range(count):
        both = attns[m][tokens:, : 2 * heads].astype(F32)
        table = table + both[:, :heads] + both[:, heads:]
    table_ref[...] = table


def mixed_body(masks, head_ref, attn_ref, w_ref, send_ref, keep_ref):
    me = head_ref[0]
    tokens, width = send_ref.shape[1:]
    attn = attn_ref[:tokens, :]
    half = len(masks) // 2
    for n, m in enumerate(masks[half:] + masks[:half]):
        start = pl.multiple_of((me ^ m) * width, width)
        out_ref = send_ref if n < half else keep_ref
        out_ref[n % half] = nn(attn, w_ref[:, pl.ds(start, width)]).astype(BF16)


def final_body(heads, count, seq_ref, k_ref, v_ref, dk_in, dv_in, *rest):
    terms = rest[:count]
    dk_ref, dv_ref = rest[count:]
    me = seq_ref[0]
    size = k_ref.shape[1] // heads
    for h in range(heads):
        cols = slice(h * size, (h + 1) * size)
        u = jnp.zeros((size, size), F32)
        for b in range(count):
            owned = (1 - ((me >> b) & 1)).astype(F32)
            u = u + owned * terms[b][0, h * size : (h + 1) * size, :].astype(F32)
        u = u.astype(BF16)
        dk_ref[:, cols] = (dk_in[:, cols] + nt(v_ref[:, cols], u)).astype(BF16)
        dv_ref[:, cols] = (dv_in[:, cols] + nn(k_ref[:, cols], u)).astype(BF16)


def swap(value, axis, mask):
    pairs = [(i, i ^ mask) for i in range(lax.axis_size(axis))]
    return lax.ppermute(value, axis, pairs)


def one_way(value, axis, mask, up):
    n = lax.axis_size(axis)
    pairs = [(i, i ^ mask) for i in range(n) if (i & mask == 0) == up]
    return lax.ppermute(value, axis, pairs)


def reduce_blocks(send, keep, axis, bits, name):
    parts = [keep]
    for n, bit in enumerate(bits):
        if n > 0:
            half = parts[0].shape[0] // 2
            send = sum(part[half:].astype(F32) for part in parts).astype(BF16)
            parts = [part[:half] for part in parts]
        with jax.named_scope(f"{name}_{n}"):
            parts.append(swap(send, axis, 1 << bit))
    return sum(part[0].astype(F32) for part in parts)


def bit_order(bits):
    masks = [0]
    for bit in reversed(range(bits)):
        masks = masks + [m | (1 << bit) for m in masks]
    return masks


def per_device(queries, keys, values, level_table, level_code, out_weight, cotangent):
    tokens, cols = queries.shape
    heads = level_table.shape[1]
    codes = level_table.shape[0]
    size = cols // heads
    width = out_weight.shape[1]
    spans = tokens // SPAN
    local_bits = spans.bit_length() - 1
    seq_count = lax.axis_size("seq")
    seq_bits = seq_count.bit_length() - 1
    head_count = lax.axis_size("head")
    head_bits = head_count.bit_length() - 1
    local_levels = 1 + local_bits
    levels = local_levels + seq_bits
    group_bits = min(2, seq_bits - 1)
    group = 1 << group_bits
    high_bits = seq_bits - group_bits
    rows = width // seq_count
    scales = [1.0 / math.sqrt(SPAN * 2 ** max(l - 1, 0)) for l in range(levels)]
    seq_me = lax.axis_index("seq").astype(jnp.int32)
    head_me = lax.axis_index("head").astype(jnp.int32)
    seq_one = seq_me.reshape(1)
    head_one = head_me.reshape(1)

    blocks = {0: cotangent}
    for bit in reversed(range(head_bits)):
        for m in list(blocks):
            with jax.named_scope(f"gather_{m | (1 << bit)}"):
                blocks[m | (1 << bit)] = swap(blocks[m], "head", 1 << bit)

    (state,) = local_call(
        functools.partial(state_body, heads),
        [shaped((cols, size), BF16)],
        [keys, values],
        flops=2 * tokens * cols * size,
        name="state",
    )
    coef, hot = local_call(
        functools.partial(coef_body, levels, scales),
        [shaped((tokens, levels * heads), F32), shaped((levels * codes, tokens), BF16)],
        [level_code.T, level_table.T],
        flops=4 * tokens * levels * codes * heads,
        name="coef",
    )
    found = []
    block_state = state
    for bit in range(seq_bits):
        with jax.named_scope(f"state_{bit}"):
            if bit == seq_bits - 1:
                found.append(one_way(block_state, "seq", 1 << bit, True))
            else:
                got = swap(block_state, "seq", 1 << bit)
                found.append(got)
        if bit < seq_bits - 1:
            block_state = (block_state.astype(F32) + got.astype(F32)).astype(BF16)

    aligned = rows % 128 == 0
    kept = [shaped((tokens, width // group), BF16)] * group if aligned else [shaped((tokens, width), BF16)]
    g, terms, *picked = local_call(
        functools.partial(grad_body, heads, local_levels, levels, head_count, group, rows),
        [shaped((tokens, cols), BF16), shaped((seq_bits, cols, size), BF16)] + kept,
        [head_one, seq_one] + [blocks[m] for m in range(head_count)] + [out_weight, queries, coef],
        scalars=2,
        flops=2 * tokens * cols * width,
        scratch=[pltpu.VMEM((tokens, width), BF16)],
        name="grad",
    )
    if not aligned:
        split = picked[0].reshape(tokens, seq_count // group, group, rows)
        picked = [
            lax.dynamic_index_in_dim(split, (seq_me & (group - 1)) ^ m, 2, False).reshape(tokens, width // group)
            for m in range(group)
        ]
    term_parts = []
    for bit in range(seq_bits):
        with jax.named_scope(f"terms_{bit}"):
            if bit == seq_bits - 1:
                got = one_way(terms, "seq", 1 << bit, False)
            else:
                got = swap(terms, "seq", 1 << bit)
        term_parts.append(got)
        if bit < seq_bits - 1:
            terms = (terms[1:].astype(F32) + got[1:].astype(F32)).astype(BF16)
    for m in range(1, group):
        with jax.named_scope(f"rows_{m}"):
            picked[m] = swap(picked[m], "seq", m)

    lev_shape = shaped((tokens, 128 * pl.cdiv(levels * heads, 128)), F32)
    attn_in, dq_in, dk_in, dv_in, lev = local_call(
        functools.partial(inner_body, heads, local_levels, scales),
        [shaped((tokens, cols), F32)] * 4 + [lev_shape],
        [queries, keys, values, g, coef],
        flops=12 * tokens * tokens * cols,
        name="inner",
    )
    table_norm = 1.0 / math.sqrt(tokens * seq_count * levels)
    if levels - 1 > local_levels:
        attn_in, dq_in, lev = local_call(
            functools.partial(outer_body, heads, local_levels, range(local_levels, levels - 1), levels, scales, None),
            [shaped((tokens, cols), F32)] * 2 + [lev_shape],
            [seq_one, queries, g, coef, attn_in, dq_in, lev] + found[:-1],
            scalars=1,
            flops=4 * tokens * cols * size * (seq_bits - 1),
            name="middle",
        )
    attn, query_grad = local_call(
        functools.partial(outer_body, heads, local_levels, [levels - 1], levels, scales, table_norm),
        [shaped((tokens + codes, cols), BF16), shaped((tokens, cols), BF16)],
        [seq_one, queries, g, coef, attn_in, dq_in, lev, found[-1], hot],
        scalars=1,
        flops=4 * tokens * cols * size,
        name="outer",
    )
    attns = [attn]
    for m in range(1, group):
        with jax.named_scope(f"attn_{m}"):
            attns.append(swap(attn, "seq", m))

    masks_m = bit_order(head_bits)
    send_shape = shaped((head_count // 2, tokens, width // head_count), BF16)
    send, keep = local_call(
        functools.partial(mixed_body, masks_m),
        [send_shape, send_shape],
        [head_one, attn, out_weight],
        scalars=1,
        flops=2 * tokens * cols * width,
        name="mixed",
    )
    mixed = reduce_blocks(send, keep, "head", range(head_bits), "mixed").astype(BF16)

    weight_norm = 1.0 / math.sqrt(tokens * seq_count)
    masks_w = bit_order(high_bits)
    half = len(masks_w) // 2

    def weight_part(masks, dtype, name):
        return local_call(
            functools.partial(weight_body, masks, weight_norm, group_bits, heads),
            [shaped((half, rows, cols), dtype), shaped((codes, heads), F32)],
            [seq_one] + picked + attns,
            scalars=1,
            flops=tokens * cols * width,
            scratch=[] if aligned else [pltpu.VMEM((width // group, cols), F32)],
            name=name,
        )

    weight_send, table_grad = weight_part(masks_w[half:], BF16, "weight_send")
    weight_keep, _ = weight_part(masks_w[:half], F32, "weight_keep")
    out_weight_grad = reduce_blocks(weight_send, weight_keep, "seq", range(group_bits, seq_bits), "weight")
    for bit in range(group_bits, seq_bits):
        with jax.named_scope(f"table_{bit}"):
            table_grad = table_grad + swap(table_grad, "seq", 1 << bit)

    key_grad, value_grad = local_call(
        functools.partial(final_body, heads, seq_bits),
        [shaped((tokens, cols), BF16)] * 2,
        [seq_one, keys, values, dk_in, dv_in] + term_parts,
        scalars=1,
        flops=4 * tokens * cols * size,
        name="final",
    )
    return mixed, out_weight_grad, query_grad, key_grad, value_grad, table_grad


def solution(mesh):
    placed = (
        P("seq", "head"),
        P("seq", "head"),
        P("seq", "head"),
        P(None, "head"),
        P("seq", None),
        P("head", None),
        P("seq", "head"),
    )
    return jax.shard_map(
        per_device,
        mesh=mesh,
        in_specs=placed,
        out_specs=(
            P("seq", "head"),
            P("seq", "head"),
            P("seq", "head"),
            P("seq", "head"),
            P("seq", "head"),
            P(None, "head"),
        ),
        check_vma=False,
    )
```

```python
import functools
import math

import jax
import jax.numpy as jnp
from jax import lax
from jax.experimental import pallas as pl
from jax.experimental.pallas import tpu as pltpu
from jax.sharding import PartitionSpec as P


SPAN = 64
F32 = jnp.float32
BF16 = jnp.bfloat16

VMEM_SPEC = pl.BlockSpec(memory_space=pltpu.VMEM)
SMEM_SPEC = pl.BlockSpec(memory_space=pltpu.SMEM)


def nn(left, right):
    return lax.dot_general(left, right, (((1,), (0,)), ((), ())), preferred_element_type=F32)


def nt(left, right):
    return lax.dot_general(left, right, (((1,), (1,)), ((), ())), preferred_element_type=F32)


def tn(left, right):
    return lax.dot_general(left, right, (((0,), (0,)), ((), ())), preferred_element_type=F32)


def local_call(body, outs, ins, scalars=0, flops=0, scratch=()):
    moved = sum(math.prod(o.shape) * o.dtype.itemsize for o in outs)
    moved += sum(math.prod(a.shape) * a.dtype.itemsize for a in ins)
    return pl.pallas_call(
        body,
        out_shape=tuple(outs),
        in_specs=[SMEM_SPEC] * scalars + [VMEM_SPEC] * (len(ins) - scalars),
        out_specs=tuple(VMEM_SPEC for _ in outs),
        scratch_shapes=scratch,
        cost_estimate=pl.CostEstimate(flops=flops, bytes_accessed=moved, transcendentals=0),
    )(*ins)


def shaped(shape, dtype):
    return jax.ShapeDtypeStruct(shape, dtype)


def state_body(heads, k_ref, v_ref, d_ref):
    size = k_ref.shape[1] // heads
    for h in range(heads):
        cols = slice(h * size, (h + 1) * size)
        d_ref[h * size : (h + 1) * size, :] = tn(k_ref[:, cols], v_ref[:, cols]).astype(BF16)


def level_masks(tokens, local_levels):
    row = lax.broadcasted_iota(jnp.int32, (tokens, tokens), 0)
    col = lax.broadcasted_iota(jnp.int32, (tokens, tokens), 1)
    apart = (row // SPAN) ^ (col // SPAN)
    causal = col <= row
    masks = [causal & (apart == 0)]
    for l in range(1, local_levels):
        masks.append(causal & ((apart >> (l - 1)) == 1))
    return masks


def level_weight(masks, coef_ref, heads, h):
    weight = jnp.zeros(masks[0].shape, F32)
    for l, mask in enumerate(masks):
        weight = jnp.where(mask, coef_ref[:, l * heads + h : l * heads + h + 1], weight)
    return weight


def inner_body(local_levels, scales, q_ref, k_ref, v_ref, code_ref, table_ref, attn_ref, coef_ref, hot_ref):
    heads, codes = table_ref.shape
    table = table_ref[...]
    high = table.astype(BF16)
    low = (table - high.astype(F32)).astype(BF16)
    tokens = code_ref.shape[1]
    size = q_ref.shape[1] // heads
    row = lax.broadcasted_iota(jnp.int32, (codes, tokens), 0)
    for l in range(len(scales)):
        hot = jnp.where(row == code_ref[l : l + 1, :], 1.0, 0.0).astype(BF16)
        hot_ref[l * codes : (l + 1) * codes, :] = hot
        lam = lax.dot_general(hot, high, (((0,), (1,)), ((), ())), preferred_element_type=F32)
        lam = lam + lax.dot_general(hot, low, (((0,), (1,)), ((), ())), preferred_element_type=F32)
        coef_ref[:, l * heads : (l + 1) * heads] = lam * scales[l]
    masks = level_masks(tokens, local_levels)
    for h in range(heads):
        cols = slice(h * size, (h + 1) * size)
        scores = nt(q_ref[:, cols], k_ref[:, cols]) * level_weight(masks, coef_ref, heads, h)
        attn_ref[:, cols] = nn(scores.astype(BF16), v_ref[:, cols])


def grad_body(heads, local_levels, levels, count, group, rows, *refs):
    head_ref, seq_ref = refs[:2]
    blocks = refs[2 : 2 + count]
    w_ref, q_ref, coef_ref, g_ref, t_ref = refs[2 + count : 7 + count]
    picked = refs[7 + count : -1]
    full_ref = refs[-1]
    me = head_ref[0]
    width = blocks[0].shape[1]
    size = q_ref.shape[1] // heads
    total = None
    for m in range(count):
        start = pl.multiple_of((me ^ m) * width, width)
        block = blocks[m][...]
        full_ref[:, pl.ds(start, width)] = block
        part = nt(block, w_ref[:, pl.ds(start, width)])
        total = part if total is None else total + part
    g = total.astype(BF16)
    g_ref[...] = g
    for l in range(local_levels, levels):
        for h in range(heads):
            cols = slice(h * size, (h + 1) * size)
            scaled = (g[:, cols].astype(F32) * coef_ref[:, l * heads + h : l * heads + h + 1]).astype(BF16)
            t_ref[l - local_levels, h * size : (h + 1) * size, :] = tn(q_ref[:, cols], scaled).astype(BF16)
    if len(picked) == 1:
        picked[0][...] = full_ref[...]
        return
    low = seq_ref[0] & (group - 1)
    for m in range(group):
        for n in range(picked[m].shape[1] // rows):
            start = pl.multiple_of((n * group + (low ^ m)) * rows, rows)
            picked[m][:, n * rows : (n + 1) * rows] = full_ref[:, pl.ds(start, rows)]


def outer_body(heads, local_levels, seq_ref, q_ref, coef_ref, attn_in, *rest):
    states, attn_ref = rest[:-1], rest[-1]
    me = seq_ref[0]
    size = q_ref.shape[1] // heads
    for h in range(heads):
        cols = slice(h * size, (h + 1) * size)
        q = q_ref[:, cols]
        attn = attn_in[:, cols]
        for b, state_ref in enumerate(states):
            owned = ((me >> b) & 1).astype(F32)
            place = (local_levels + b) * heads + h
            state = state_ref[h * size : (h + 1) * size, :]
            attn = attn + coef_ref[:, place : place + 1] * owned * nn(q, state)
        attn_ref[:, cols] = attn.astype(BF16)


def back_body(heads, local_levels, scales, norm, seq_ref, q_ref, k_ref, v_ref, g_ref, coef_ref, hot_ref, *rest):
    states = rest[: len(scales) - local_levels]
    dq_ref, dk_ref, dv_ref, table_ref = rest[len(scales) - local_levels :]
    me = seq_ref[0]
    tokens = q_ref.shape[0]
    size = q_ref.shape[1] // heads
    codes = table_ref.shape[0]
    masks = level_masks(tokens, local_levels)
    lanes = 128 * pl.cdiv(len(scales) * heads, 128)
    lane = lax.broadcasted_iota(jnp.int32, (tokens, lanes), 1)
    lev = jnp.zeros((tokens, lanes), F32)
    for h in range(heads):
        cols = slice(h * size, (h + 1) * size)
        q, k, v, g = q_ref[:, cols], k_ref[:, cols], v_ref[:, cols], g_ref[:, cols]
        weight = level_weight(masks, coef_ref, heads, h)
        scores = nt(q, k)
        grads = nt(g, v)
        both = scores * grads
        for l in range(local_levels):
            part = jnp.sum(jnp.where(masks[l], both, 0.0), axis=1, keepdims=True) * scales[l]
            lev = jnp.where(lane == l * heads + h, part, lev)
        scores = (scores * weight).astype(BF16)
        grads = (grads * weight).astype(BF16)
        dk_ref[:, cols] = tn(grads, q)
        dv_ref[:, cols] = tn(scores, g)
        dq = nn(grads, k)
        qf = q.astype(F32)
        for b, state_ref in enumerate(states):
            owned = ((me >> b) & 1).astype(F32)
            place = (local_levels + b) * heads + h
            back = nt(g, state_ref[h * size : (h + 1) * size, :])
            dq = dq + coef_ref[:, place : place + 1] * owned * back
            part = jnp.sum(qf * back, axis=1, keepdims=True) * (owned * scales[local_levels + b])
            lev = jnp.where(lane == place, part, lev)
        dq_ref[:, cols] = dq.astype(BF16)
    high = lev.astype(BF16)
    low = (lev - high.astype(F32)).astype(BF16)
    total = jnp.zeros((codes, heads), F32)
    for l in range(len(scales)):
        hot = hot_ref[l * codes : (l + 1) * codes, :]
        pick = slice(l * heads, (l + 1) * heads)
        total = total + nn(hot, high[:, pick]) + nn(hot, low[:, pick])
    table_ref[...] = total * norm


def weight_body(masks, scale, group_bits, seq_ref, *refs):
    count = 1 << group_bits
    picked, attns, out_ref = refs[:count], refs[count : 2 * count], refs[2 * count]
    scratch = refs[2 * count + 1 :]
    me = seq_ref[0] >> group_bits
    rows = out_ref.shape[1]

    def product(cols):
        total = None
        for m in range(count):
            part = tn(picked[m][:, cols], attns[m][...])
            total = part if total is None else total + part
        return total * scale

    if scratch:
        scratch[0][...] = product(slice(None))
    for n, m in enumerate(masks):
        start = pl.multiple_of((me ^ m) * rows, rows)
        total = scratch[0][pl.ds(start, rows), :] if scratch else product(pl.ds(start, rows))
        out_ref[n] = total.astype(out_ref.dtype)


def mixed_body(masks, head_ref, attn_ref, w_ref, send_ref, keep_ref):
    me = head_ref[0]
    width = send_ref.shape[2]
    attn = attn_ref[...]
    half = len(masks) // 2
    for n, m in enumerate(masks[half:] + masks[:half]):
        start = pl.multiple_of((me ^ m) * width, width)
        out_ref = send_ref if n < half else keep_ref
        out_ref[n % half] = nn(attn, w_ref[:, pl.ds(start, width)]).astype(BF16)


def final_body(heads, count, seq_ref, k_ref, v_ref, dk_in, dv_in, *rest):
    terms = rest[:count]
    dk_ref, dv_ref = rest[count:]
    me = seq_ref[0]
    size = k_ref.shape[1] // heads
    for h in range(heads):
        cols = slice(h * size, (h + 1) * size)
        u = jnp.zeros((size, size), F32)
        for b in range(count):
            owned = (1 - ((me >> b) & 1)).astype(F32)
            u = u + owned * terms[b][0, h * size : (h + 1) * size, :].astype(F32)
        u = u.astype(BF16)
        dk_ref[:, cols] = (dk_in[:, cols] + nt(v_ref[:, cols], u)).astype(BF16)
        dv_ref[:, cols] = (dv_in[:, cols] + nn(k_ref[:, cols], u)).astype(BF16)


def swap(value, axis, mask):
    pairs = [(i, i ^ mask) for i in range(lax.axis_size(axis))]
    return lax.ppermute(value, axis, pairs)


def one_way(value, axis, mask, up):
    n = lax.axis_size(axis)
    pairs = [(i, i ^ mask) for i in range(n) if (i & mask == 0) == up]
    return lax.ppermute(value, axis, pairs)


def reduce_blocks(send, keep, axis, bits):
    parts = [keep]
    for n, bit in enumerate(bits):
        if n > 0:
            half = parts[0].shape[0] // 2
            send = sum(part[half:].astype(F32) for part in parts).astype(BF16)
            parts = [part[:half] for part in parts]
        parts.append(swap(send, axis, 1 << bit))
    return sum(part[0].astype(F32) for part in parts)


def bit_order(bits):
    masks = [0]
    for bit in reversed(range(bits)):
        masks = masks + [m | (1 << bit) for m in masks]
    return masks


def per_device(queries, keys, values, level_table, level_code, out_weight, cotangent):
    tokens, cols = queries.shape
    heads = level_table.shape[1]
    codes = level_table.shape[0]
    size = cols // heads
    width = out_weight.shape[1]
    spans = tokens // SPAN
    local_bits = spans.bit_length() - 1
    seq_count = lax.axis_size("seq")
    seq_bits = seq_count.bit_length() - 1
    head_count = lax.axis_size("head")
    head_bits = head_count.bit_length() - 1
    local_levels = 1 + local_bits
    levels = local_levels + seq_bits
    group_bits = min(2, seq_bits - 1)
    group = 1 << group_bits
    high_bits = seq_bits - group_bits
    rows = width // seq_count
    scales = [1.0 / math.sqrt(SPAN * 2 ** max(l - 1, 0)) for l in range(levels)]
    seq_me = lax.axis_index("seq").astype(jnp.int32)
    head_me = lax.axis_index("head").astype(jnp.int32)
    seq_one = seq_me.reshape(1)
    head_one = head_me.reshape(1)

    blocks = {0: cotangent}
    for bit in reversed(range(head_bits)):
        for m in list(blocks):
            blocks[m | (1 << bit)] = swap(blocks[m], "head", 1 << bit)

    (state,) = local_call(
        functools.partial(state_body, heads),
        [shaped((cols, size), BF16)],
        [keys, values],
        flops=2 * tokens * cols * size,
    )
    attn_in, coef, hot = local_call(
        functools.partial(inner_body, local_levels, scales),
        [
            shaped((tokens, cols), F32),
            shaped((tokens, levels * heads), F32),
            shaped((levels * codes, tokens), BF16),
        ],
        [queries, keys, values, level_code.T, level_table.T],
        flops=4 * tokens * tokens * cols,
    )
    found = []
    block_state = state
    for bit in range(seq_bits):
        if bit == seq_bits - 1:
            found.append(one_way(block_state, "seq", 1 << bit, True))
        else:
            got = swap(block_state, "seq", 1 << bit)
            found.append(got)
        if bit < seq_bits - 1:
            block_state = (block_state.astype(F32) + got.astype(F32)).astype(BF16)

    aligned = rows % 128 == 0
    kept = [shaped((tokens, width // group), BF16)] * group if aligned else [shaped((tokens, width), BF16)]
    g, terms, *picked = local_call(
        functools.partial(grad_body, heads, local_levels, levels, head_count, group, rows),
        [shaped((tokens, cols), BF16), shaped((seq_bits, cols, size), BF16)] + kept,
        [head_one, seq_one] + [blocks[m] for m in range(head_count)] + [out_weight, queries, coef],
        scalars=2,
        flops=2 * tokens * cols * width,
        scratch=[pltpu.VMEM((tokens, width), BF16)],
    )
    if not aligned:
        split = picked[0].reshape(tokens, seq_count // group, group, rows)
        picked = [
            lax.dynamic_index_in_dim(split, (seq_me & (group - 1)) ^ m, 2, False).reshape(tokens, width // group)
            for m in range(group)
        ]
    term_parts = []
    for bit in range(seq_bits):
        if bit == seq_bits - 1:
            got = one_way(terms, "seq", 1 << bit, False)
        else:
            got = swap(terms, "seq", 1 << bit)
        term_parts.append(got)
        if bit < seq_bits - 1:
            terms = (terms[1:].astype(F32) + got[1:].astype(F32)).astype(BF16)
    for m in range(1, group):
        picked[m] = swap(picked[m], "seq", m)

    (attn,) = local_call(
        functools.partial(outer_body, heads, local_levels),
        [shaped((tokens, cols), BF16)],
        [seq_one, queries, coef, attn_in] + found,
        scalars=1,
        flops=2 * tokens * cols * size * seq_bits,
    )
    table_norm = 1.0 / math.sqrt(tokens * seq_count * levels)
    query_grad, dk_in, dv_in, table_grad = local_call(
        functools.partial(back_body, heads, local_levels, scales, table_norm),
        [shaped((tokens, cols), BF16)] + [shaped((tokens, cols), F32)] * 2 + [shaped((codes, heads), F32)],
        [seq_one, queries, keys, values, g, coef, hot] + found,
        scalars=1,
        flops=10 * tokens * tokens * cols,
    )
    for bit in range(seq_bits):
        table_grad = table_grad + swap(table_grad, "seq", 1 << bit)
    attns = [attn]
    for m in range(1, group):
        attns.append(swap(attn, "seq", m))

    masks_m = bit_order(head_bits)
    send_shape = shaped((head_count // 2, tokens, width // head_count), BF16)
    send, keep = local_call(
        functools.partial(mixed_body, masks_m),
        [send_shape, send_shape],
        [head_one, attn, out_weight],
        scalars=1,
        flops=2 * tokens * cols * width,
    )
    mixed = reduce_blocks(send, keep, "head", range(head_bits)).astype(BF16)

    weight_norm = 1.0 / math.sqrt(tokens * seq_count)
    masks_w = bit_order(high_bits)
    half = len(masks_w) // 2

    def weight_part(masks, dtype):
        return local_call(
            functools.partial(weight_body, masks, weight_norm, group_bits),
            [shaped((half, rows, cols), dtype)],
            [seq_one] + picked + attns,
            scalars=1,
            flops=tokens * cols * width,
            scratch=[] if aligned else [pltpu.VMEM((width // group, cols), F32)],
        )

    (weight_send,) = weight_part(masks_w[half:], BF16)
    (weight_keep,) = weight_part(masks_w[:half], F32)
    out_weight_grad = reduce_blocks(weight_send, weight_keep, "seq", range(group_bits, seq_bits))

    key_grad, value_grad = local_call(
        functools.partial(final_body, heads, seq_bits),
        [shaped((tokens, cols), BF16)] * 2,
        [seq_one, keys, values, dk_in, dv_in] + term_parts,
        scalars=1,
        flops=4 * tokens * cols * size,
    )
    return mixed, out_weight_grad, query_grad, key_grad, value_grad, table_grad


def solution(mesh):
    placed = (
        P("seq", "head"),
        P("seq", "head"),
        P("seq", "head"),
        P(None, "head"),
        P("seq", None),
        P("head", None),
        P("seq", "head"),
    )

    return jax.shard_map(
        per_device,
        mesh=mesh,
        in_specs=placed,
        out_specs=(
            P("seq", "head"),
            P("seq", "head"),
            P("seq", "head"),
            P("seq", "head"),
            P("seq", "head"),
            P(None, "head"),
        ),
        check_vma=False,
    )
```

```python
import functools
import math

import jax
import jax.numpy as jnp
from jax import lax
from jax.experimental import pallas as pl
from jax.experimental.pallas import tpu as pltpu
from jax.sharding import PartitionSpec as P


SPAN = 64
F32 = jnp.float32
BF16 = jnp.bfloat16

VMEM_SPEC = pl.BlockSpec(memory_space=pltpu.VMEM)
SMEM_SPEC = pl.BlockSpec(memory_space=pltpu.SMEM)


def nn(left, right):
    return lax.dot_general(left, right, (((1,), (0,)), ((), ())), preferred_element_type=F32)


def nt(left, right):
    return lax.dot_general(left, right, (((1,), (1,)), ((), ())), preferred_element_type=F32)


def tn(left, right):
    return lax.dot_general(left, right, (((0,), (0,)), ((), ())), preferred_element_type=F32)


def local_call(body, outs, ins, scalars=0, flops=0, scratch=()):
    moved = sum(math.prod(o.shape) * o.dtype.itemsize for o in outs)
    moved += sum(math.prod(a.shape) * a.dtype.itemsize for a in ins)
    return pl.pallas_call(
        body,
        out_shape=tuple(outs),
        in_specs=[SMEM_SPEC] * scalars + [VMEM_SPEC] * (len(ins) - scalars),
        out_specs=tuple(VMEM_SPEC for _ in outs),
        scratch_shapes=scratch,
        cost_estimate=pl.CostEstimate(flops=flops, bytes_accessed=moved, transcendentals=0),
    )(*ins)


def shaped(shape, dtype):
    return jax.ShapeDtypeStruct(shape, dtype)


def state_body(heads, k_ref, v_ref, d_ref):
    size = k_ref.shape[1] // heads
    for h in range(heads):
        cols = slice(h * size, (h + 1) * size)
        d_ref[h * size : (h + 1) * size, :] = tn(k_ref[:, cols], v_ref[:, cols]).astype(BF16)


def level_masks(tokens, local_levels):
    row = lax.broadcasted_iota(jnp.int32, (tokens, tokens), 0)
    col = lax.broadcasted_iota(jnp.int32, (tokens, tokens), 1)
    apart = (row // SPAN) ^ (col // SPAN)
    causal = col <= row
    masks = [causal & (apart == 0)]
    for l in range(1, local_levels):
        masks.append(causal & ((apart >> (l - 1)) == 1))
    return masks


def level_weight(masks, coef_ref, heads, h):
    weight = jnp.zeros(masks[0].shape, F32)
    for l, mask in enumerate(masks):
        weight = jnp.where(mask, coef_ref[:, l * heads + h : l * heads + h + 1], weight)
    return weight


def inner_body(local_levels, scales, q_ref, k_ref, v_ref, code_ref, table_ref, attn_ref, coef_ref, hot_ref):
    heads, codes = table_ref.shape
    table = table_ref[...]
    high = table.astype(BF16)
    low = (table - high.astype(F32)).astype(BF16)
    tokens = code_ref.shape[1]
    size = q_ref.shape[1] // heads
    row = lax.broadcasted_iota(jnp.int32, (codes, tokens), 0)
    for l in range(len(scales)):
        hot = jnp.where(row == code_ref[l : l + 1, :], 1.0, 0.0).astype(BF16)
        hot_ref[l * codes : (l + 1) * codes, :] = hot
        lam = lax.dot_general(hot, high, (((0,), (1,)), ((), ())), preferred_element_type=F32)
        lam = lam + lax.dot_general(hot, low, (((0,), (1,)), ((), ())), preferred_element_type=F32)
        coef_ref[:, l * heads : (l + 1) * heads] = lam * scales[l]
    masks = level_masks(tokens, local_levels)
    for h in range(heads):
        cols = slice(h * size, (h + 1) * size)
        scores = nt(q_ref[:, cols], k_ref[:, cols]) * level_weight(masks, coef_ref, heads, h)
        attn_ref[:, cols] = nn(scores.astype(BF16), v_ref[:, cols])


def grad_body(heads, local_levels, levels, count, group, rows, *refs):
    head_ref, seq_ref = refs[:2]
    blocks = refs[2 : 2 + count]
    w_ref, q_ref, coef_ref, g_ref, t_ref = refs[2 + count : 7 + count]
    picked = refs[7 + count : -1]
    full_ref = refs[-1]
    me = head_ref[0]
    width = blocks[0].shape[1]
    size = q_ref.shape[1] // heads
    total = None
    for m in range(count):
        start = pl.multiple_of((me ^ m) * width, width)
        block = blocks[m][...]
        full_ref[:, pl.ds(start, width)] = block
        part = nt(block, w_ref[:, pl.ds(start, width)])
        total = part if total is None else total + part
    g = total.astype(BF16)
    g_ref[...] = g
    for l in range(local_levels, levels):
        for h in range(heads):
            cols = slice(h * size, (h + 1) * size)
            scaled = (g[:, cols].astype(F32) * coef_ref[:, l * heads + h : l * heads + h + 1]).astype(BF16)
            t_ref[l - local_levels, h * size : (h + 1) * size, :] = tn(q_ref[:, cols], scaled).astype(BF16)
    if len(picked) == 1:
        picked[0][...] = full_ref[...]
        return
    low = seq_ref[0] & (group - 1)
    for m in range(group):
        for n in range(picked[m].shape[1] // rows):
            start = pl.multiple_of((n * group + (low ^ m)) * rows, rows)
            picked[m][:, n * rows : (n + 1) * rows] = full_ref[:, pl.ds(start, rows)]


def outer_body(heads, local_levels, seq_ref, q_ref, coef_ref, attn_in, *rest):
    states, attn_ref = rest[:-1], rest[-1]
    me = seq_ref[0]
    size = q_ref.shape[1] // heads
    for h in range(heads):
        cols = slice(h * size, (h + 1) * size)
        q = q_ref[:, cols]
        attn = attn_in[:, cols]
        for b, state_ref in enumerate(states):
            owned = ((me >> b) & 1).astype(F32)
            place = (local_levels + b) * heads + h
            state = state_ref[h * size : (h + 1) * size, :]
            attn = attn + coef_ref[:, place : place + 1] * owned * nn(q, state)
        attn_ref[:, cols] = attn.astype(BF16)


def back_body(heads, local_levels, scales, norm, seq_ref, q_ref, k_ref, v_ref, g_ref, coef_ref, hot_ref, *rest):
    states = rest[: len(scales) - local_levels]
    dq_ref, dk_ref, dv_ref, table_ref = rest[len(scales) - local_levels :]
    me = seq_ref[0]
    tokens = q_ref.shape[0]
    size = q_ref.shape[1] // heads
    codes = table_ref.shape[0]
    masks = level_masks(tokens, local_levels)
    lanes = 128 * pl.cdiv(len(scales) * heads, 128)
    lane = lax.broadcasted_iota(jnp.int32, (tokens, lanes), 1)
    lev = jnp.zeros((tokens, lanes), F32)
    for h in range(heads):
        cols = slice(h * size, (h + 1) * size)
        q, k, v, g = q_ref[:, cols], k_ref[:, cols], v_ref[:, cols], g_ref[:, cols]
        weight = level_weight(masks, coef_ref, heads, h)
        scores = nt(q, k)
        grads = nt(g, v)
        both = scores * grads
        for l in range(local_levels):
            part = jnp.sum(jnp.where(masks[l], both, 0.0), axis=1, keepdims=True) * scales[l]
            lev = jnp.where(lane == l * heads + h, part, lev)
        scores = (scores * weight).astype(BF16)
        grads = (grads * weight).astype(BF16)
        dk_ref[:, cols] = tn(grads, q)
        dv_ref[:, cols] = tn(scores, g)
        dq = nn(grads, k)
        qf = q.astype(F32)
        for b, state_ref in enumerate(states):
            owned = ((me >> b) & 1).astype(F32)
            place = (local_levels + b) * heads + h
            back = nt(g, state_ref[h * size : (h + 1) * size, :])
            dq = dq + coef_ref[:, place : place + 1] * owned * back
            part = jnp.sum(qf * back, axis=1, keepdims=True) * (owned * scales[local_levels + b])
            lev = jnp.where(lane == place, part, lev)
        dq_ref[:, cols] = dq.astype(BF16)
    high = lev.astype(BF16)
    low = (lev - high.astype(F32)).astype(BF16)
    total = jnp.zeros((codes, heads), F32)
    for l in range(len(scales)):
        hot = hot_ref[l * codes : (l + 1) * codes, :]
        pick = slice(l * heads, (l + 1) * heads)
        total = total + nn(hot, high[:, pick]) + nn(hot, low[:, pick])
    table_ref[...] = total * norm


def weight_body(masks, scale, group_bits, seq_ref, *refs):
    count = 1 << group_bits
    picked, attns, out_ref = refs[:count], refs[count : 2 * count], refs[2 * count]
    scratch = refs[2 * count + 1 :]
    me = seq_ref[0] >> group_bits
    rows = out_ref.shape[1]

    def product(cols):
        total = None
        for m in range(count):
            part = tn(picked[m][:, cols], attns[m][...])
            total = part if total is None else total + part
        return total * scale

    if scratch:
        scratch[0][...] = product(slice(None))
    for n, m in enumerate(masks):
        start = pl.multiple_of((me ^ m) * rows, rows)
        total = scratch[0][pl.ds(start, rows), :] if scratch else product(pl.ds(start, rows))
        out_ref[n] = total.astype(out_ref.dtype)


def mixed_body(masks, head_ref, attn_ref, w_ref, send_ref, keep_ref):
    me = head_ref[0]
    width = send_ref.shape[2]
    attn = attn_ref[...]
    half = len(masks) // 2
    for n, m in enumerate(masks[half:] + masks[:half]):
        start = pl.multiple_of((me ^ m) * width, width)
        out_ref = send_ref if n < half else keep_ref
        out_ref[n % half] = nn(attn, w_ref[:, pl.ds(start, width)]).astype(BF16)


def final_body(heads, count, seq_ref, k_ref, v_ref, dk_in, dv_in, *rest):
    terms = rest[:count]
    dk_ref, dv_ref = rest[count:]
    me = seq_ref[0]
    size = k_ref.shape[1] // heads
    for h in range(heads):
        cols = slice(h * size, (h + 1) * size)
        u = jnp.zeros((size, size), F32)
        for b in range(count):
            owned = (1 - ((me >> b) & 1)).astype(F32)
            u = u + owned * terms[b][0, h * size : (h + 1) * size, :].astype(F32)
        u = u.astype(BF16)
        dk_ref[:, cols] = (dk_in[:, cols] + nt(v_ref[:, cols], u)).astype(BF16)
        dv_ref[:, cols] = (dv_in[:, cols] + nn(k_ref[:, cols], u)).astype(BF16)


def swap(value, axis, mask):
    pairs = [(i, i ^ mask) for i in range(lax.axis_size(axis))]
    return lax.ppermute(value, axis, pairs)


def reduce_blocks(send, keep, axis, bits):
    parts = [keep]
    for n, bit in enumerate(bits):
        if n > 0:
            half = parts[0].shape[0] // 2
            send = sum(part[half:].astype(F32) for part in parts).astype(BF16)
            parts = [part[:half] for part in parts]
        parts.append(swap(send, axis, 1 << bit))
    return sum(part[0].astype(F32) for part in parts)


def bit_order(bits):
    masks = [0]
    for bit in reversed(range(bits)):
        masks = masks + [m | (1 << bit) for m in masks]
    return masks


def per_device(queries, keys, values, level_table, level_code, out_weight, cotangent):
    tokens, cols = queries.shape
    heads = level_table.shape[1]
    codes = level_table.shape[0]
    size = cols // heads
    width = out_weight.shape[1]
    spans = tokens // SPAN
    local_bits = spans.bit_length() - 1
    seq_count = lax.axis_size("seq")
    seq_bits = seq_count.bit_length() - 1
    head_count = lax.axis_size("head")
    head_bits = head_count.bit_length() - 1
    local_levels = 1 + local_bits
    levels = local_levels + seq_bits
    group_bits = min(2, seq_bits - 1)
    group = 1 << group_bits
    high_bits = seq_bits - group_bits
    rows = width // seq_count
    scales = [1.0 / math.sqrt(SPAN * 2 ** max(l - 1, 0)) for l in range(levels)]
    seq_me = lax.axis_index("seq").astype(jnp.int32)
    head_me = lax.axis_index("head").astype(jnp.int32)
    seq_one = seq_me.reshape(1)
    head_one = head_me.reshape(1)

    blocks = {0: cotangent}
    for bit in reversed(range(head_bits)):
        for m in list(blocks):
            blocks[m | (1 << bit)] = swap(blocks[m], "head", 1 << bit)

    (state,) = local_call(
        functools.partial(state_body, heads),
        [shaped((cols, size), BF16)],
        [keys, values],
        flops=2 * tokens * cols * size,
    )
    attn_in, coef, hot = local_call(
        functools.partial(inner_body, local_levels, scales),
        [
            shaped((tokens, cols), F32),
            shaped((tokens, levels * heads), F32),
            shaped((levels * codes, tokens), BF16),
        ],
        [queries, keys, values, level_code.T, level_table.T],
        flops=4 * tokens * tokens * cols,
    )
    found = []
    block_state = state
    for bit in range(seq_bits):
        got = swap(block_state, "seq", 1 << bit)
        found.append(got)
        if bit < seq_bits - 1:
            block_state = (block_state.astype(F32) + got.astype(F32)).astype(BF16)

    aligned = rows % 128 == 0
    kept = [shaped((tokens, width // group), BF16)] * group if aligned else [shaped((tokens, width), BF16)]
    g, terms, *picked = local_call(
        functools.partial(grad_body, heads, local_levels, levels, head_count, group, rows),
        [shaped((tokens, cols), BF16), shaped((seq_bits, cols, size), BF16)] + kept,
        [head_one, seq_one] + [blocks[m] for m in range(head_count)] + [out_weight, queries, coef],
        scalars=2,
        flops=2 * tokens * cols * width,
        scratch=[pltpu.VMEM((tokens, width), BF16)],
    )
    if not aligned:
        split = picked[0].reshape(tokens, seq_count // group, group, rows)
        picked = [
            lax.dynamic_index_in_dim(split, (seq_me & (group - 1)) ^ m, 2, False).reshape(tokens, width // group)
            for m in range(group)
        ]
    term_parts = []
    for bit in range(seq_bits):
        got = swap(terms, "seq", 1 << bit)
        term_parts.append(got)
        if bit < seq_bits - 1:
            terms = (terms[1:].astype(F32) + got[1:].astype(F32)).astype(BF16)
    for m in range(1, group):
        picked[m] = swap(picked[m], "seq", m)

    (attn,) = local_call(
        functools.partial(outer_body, heads, local_levels),
        [shaped((tokens, cols), BF16)],
        [seq_one, queries, coef, attn_in] + found,
        scalars=1,
        flops=2 * tokens * cols * size * seq_bits,
    )
    table_norm = 1.0 / math.sqrt(tokens * seq_count * levels)
    query_grad, dk_in, dv_in, table_grad = local_call(
        functools.partial(back_body, heads, local_levels, scales, table_norm),
        [shaped((tokens, cols), BF16)] + [shaped((tokens, cols), F32)] * 2 + [shaped((codes, heads), F32)],
        [seq_one, queries, keys, values, g, coef, hot] + found,
        scalars=1,
        flops=10 * tokens * tokens * cols,
    )
    for bit in range(seq_bits):
        table_grad = table_grad + swap(table_grad, "seq", 1 << bit)
    attns = [attn]
    for m in range(1, group):
        attns.append(swap(attn, "seq", m))

    masks_m = bit_order(head_bits)
    send_shape = shaped((head_count // 2, tokens, width // head_count), BF16)
    send, keep = local_call(
        functools.partial(mixed_body, masks_m),
        [send_shape, send_shape],
        [head_one, attn, out_weight],
        scalars=1,
        flops=2 * tokens * cols * width,
    )
    mixed = reduce_blocks(send, keep, "head", range(head_bits)).astype(BF16)

    weight_norm = 1.0 / math.sqrt(tokens * seq_count)
    masks_w = bit_order(high_bits)
    half = len(masks_w) // 2

    def weight_part(masks, dtype):
        return local_call(
            functools.partial(weight_body, masks, weight_norm, group_bits),
            [shaped((half, rows, cols), dtype)],
            [seq_one] + picked + attns,
            scalars=1,
            flops=tokens * cols * width,
            scratch=[] if aligned else [pltpu.VMEM((width // group, cols), F32)],
        )

    (weight_send,) = weight_part(masks_w[half:], BF16)
    (weight_keep,) = weight_part(masks_w[:half], F32)
    out_weight_grad = reduce_blocks(weight_send, weight_keep, "seq", range(group_bits, seq_bits))

    key_grad, value_grad = local_call(
        functools.partial(final_body, heads, seq_bits),
        [shaped((tokens, cols), BF16)] * 2,
        [seq_one, keys, values, dk_in, dv_in] + term_parts,
        scalars=1,
        flops=4 * tokens * cols * size,
    )
    return mixed, out_weight_grad, query_grad, key_grad, value_grad, table_grad


def solution(mesh):
    placed = (
        P("seq", "head"),
        P("seq", "head"),
        P("seq", "head"),
        P(None, "head"),
        P("seq", None),
        P("head", None),
        P("seq", "head"),
    )

    return jax.shard_map(
        per_device,
        mesh=mesh,
        in_specs=placed,
        out_specs=(
            P("seq", "head"),
            P("seq", "head"),
            P("seq", "head"),
            P("seq", "head"),
            P("seq", "head"),
            P(None, "head"),
        ),
        check_vma=False,
    )
```
